256 devices in a mesh: dp: 64 (over z_lo, y, x, core), mp: 4 (over z_hi).
Axes of the slice: x: 4, y: 4, z: 8 (z_hi: 4, z_lo: 2; z = z_hi * 2 + z_lo), core: 2. Of those that a mesh axis runs over, the one named last changes fastest.
Arguments:
- pooled_rows: float32 [8192, 1152], P('dp', 'mp'), may hold values from -8 to 8
- projection: float32 [1152, 1152], P('mp'), may hold values from -0.1875 to 0.1875
- text_rows: float32 [8192, 1152], P(('dp', 'mp')), may hold values from -8 to 8
- caption_row: int32 [8192], P('dp'), may hold values from 0 to 8191, as said below
Outputs:
- pooled_grad: float32 [8192, 1152], P('dp', 'mp')
- text_grad: float32 [8192, 1152], P(('dp', 'mp'))
The draws below stay inside these ranges and needn't reach their ends.
Inputs may be any that keep to these rules, and one draw needn't show every extreme that they name: `caption_row`: every caption row is named by exactly one image. Of the 128 images of one index of dp, those whose caption row lies in the block of 128 rows of any one index (its own included) number 1 to 3; 3 is reached by some pair of indices.
All inputs are finite; a program needn't handle non-finite values.
Results may differ from the reference program's by a relative error of at most 0.0003.
Values sent between devices are 32-bit elements; how exact they have to be, the bound alone decides.
No kernel may reach another device: no remote copies, remote signals or barrier semaphores. Data moves between devices by JAX's collectives and lax.ppermute only.
A program may use at most 64 MiB of HBM per device.

```python
import math
import jax
import jax.numpy as jnp
from jax import lax

D = 1152
E = 1152
IMG_DP = 128
IMAGES = 8192
CAPB = 3


def scaled_rows(key, count, width):
    first, second, third = jax.random.split(key, 3)
    row_scale = jnp.exp(jax.random.uniform(second, (count, 1), jnp.float32, math.log(0.05), math.log(0.5)))
    column_scale = jnp.exp(jax.random.uniform(third, (1, width), jnp.float32, math.log(0.3), math.log(3.0)))
    base = jax.random.normal(first, (count, width), jnp.float32)
    return jnp.clip(base * row_scale * column_scale, -8.0, 8.0).astype(jnp.float32)


def draw_pooled_rows(key, part):
    return scaled_rows(jax.random.fold_in(key, 11), IMAGES, D)


def draw_text_rows(key, part):
    return scaled_rows(jax.random.fold_in(key, 23), IMAGES, E)


def draw_caption_row(key, part):
    shards = IMAGES // IMG_DP
    first, second, third, fourth = jax.random.split(jax.random.fold_in(key, 37), 4)
    offsets = jax.random.permutation(first, shards).astype(jnp.int32)
    base = IMG_DP // shards
    spread = CAPB - base
    half = shards // 2
    delta = jax.random.randint(second, (half,), 0, spread + 1).astype(jnp.int32)
    delta = delta.at[0].set(spread)
    amounts = jnp.concatenate([base + delta, base - delta])
    ends = jnp.cumsum(amounts)
    positions = jnp.arange(IMG_DP, dtype=jnp.int32)
    group = jnp.sum((positions[:, None] >= ends[None, :]).astype(jnp.int32), axis=1)
    sources = jnp.arange(shards, dtype=jnp.int32)
    target = (sources[:, None] + offsets[group][None, :]) % shards
    order = jax.vmap(lambda k: jax.random.permutation(k, IMG_DP).astype(jnp.int32))(jax.random.split(third, shards))
    slots = jax.vmap(lambda k: jax.random.permutation(k, IMG_DP).astype(jnp.int32))(jax.random.split(fourth, shards))
    landing = slots[target, jnp.broadcast_to(positions[None, :], (shards, IMG_DP))]
    row_value = target * IMG_DP + landing
    result = jnp.zeros((shards, IMG_DP), jnp.int32).at[sources[:, None], order].set(row_value)
    return result.reshape(IMAGES)


def steps_of(own_key, extent, pieces, low, largest):
    def one(dim, parts):
        heights = jax.random.uniform(jax.random.fold_in(jax.random.fold_in(own_key, 6), dim), (parts,), jnp.float32, low / len(pieces), largest / len(pieces))
        return jnp.repeat(jnp.exp(heights), extent[dim] // parts).reshape((-1,) + (1,) * (len(extent) - dim - 1))

    level = one(*pieces[0])
    for cut in pieces[1:]:
        level = level * one(*cut)
    return level


def bell_draw(rng, dims, scale, most, cuts=(), kind=jnp.bfloat16):
    loudness = steps_of(rng, dims, cuts, -0.22, 0.18) if cuts else 1.0
    drawn = jax.random.normal(rng, dims, jnp.float32) * scale * loudness
    return jnp.minimum(jnp.maximum(drawn, -most), most).astype(kind)


def setup_inputs(seed: int = 0) -> dict:
    splits = jax.random.split(jax.random.key(seed), 5)
    return {
        "pooled_rows": draw_pooled_rows(jax.random.fold_in(splits[4], 71), 0),
        "projection": bell_draw(splits[1], (D, E), D ** -0.5, 0.1875, ((0, 4),), jnp.float32),
        "text_rows": draw_text_rows(jax.random.fold_in(splits[4], 71), 0),
        "caption_row": draw_caption_row(jax.random.fold_in(splits[4], 71), 0),
    }


LOGIT_SCALE = 10.0
LOGIT_BIAS = -2.0
NORM_EPS = 1e-06

def product(left, right):
    return jnp.dot(left, right, precision=lax.Precision.HIGHEST, preferred_element_type=jnp.float32)

def product_nt(left, right):
    return lax.dot_general(left, right, (((1,), (1,)), ((), ())), precision=lax.Precision.HIGHEST, preferred_element_type=jnp.float32)

def product_tn(left, right):
    return lax.dot_general(left, right, (((0,), (0,)), ((), ())), precision=lax.Precision.HIGHEST, preferred_element_type=jnp.float32)

def unit_rows(raw):
    scale = lax.rsqrt(lax.optimization_barrier(jnp.sum(raw * raw, axis=1)) + NORM_EPS)
    return (raw * scale[:, None], scale)

def unit_back(unit, scale, grad):
    return scale[:, None] * (grad - unit * lax.optimization_barrier(jnp.sum(unit * grad, axis=1, keepdims=True)))

def pair_terms(images, captions, image_rows, caption_rows):
    logits = LOGIT_SCALE * product_nt(images, captions) + LOGIT_BIAS
    target = image_rows[:, None] == caption_rows[None, :]
    signs = jnp.where(target, 1.0, -1.0).astype(jnp.float32)
    weights = -signs * jax.nn.sigmoid(-signs * logits)
    return (LOGIT_SCALE * product(weights, captions), LOGIT_SCALE * product_tn(weights, images))

def reference(pooled_rows, projection, text_rows, caption_row):
    projected = product(pooled_rows, projection)
    images, image_scale = unit_rows(projected)
    captions, caption_scale = unit_rows(text_rows)
    every_row = jnp.arange(IMAGES, dtype=jnp.int32)
    blocks = IMAGES // IMG_DP

    def visit(caption_grad, inputs):
        block_images, block_rows = inputs
        image_term, caption_term = pair_terms(block_images, captions, block_rows, every_row)
        return (caption_grad + caption_term, image_term)
    caption_grad, image_grad = lax.scan(visit, jnp.zeros((IMAGES, E), jnp.float32), (images.reshape(blocks, IMG_DP, E), caption_row.reshape(blocks, IMG_DP).astype(jnp.int32)))
    image_grad = image_grad.reshape(IMAGES, E)
    pooled_grad = product(unit_back(images, image_scale, image_grad), projection.T)
    text_grad = unit_back(captions, caption_scale, caption_grad)
    return (pooled_grad, text_grad)
```

```python
import jax
import jax.numpy as jnp
from jax import lax
from jax.sharding import Mesh, PartitionSpec as P

LOGIT_SCALE = 10.0
LOGIT_BIAS = -2.0
NORM_EPS = 1e-06

SIZES = {"zl": 2, "y": 4, "x": 4, "c": 2, "zh": 4}
DP = ("zl", "y", "x", "c")
Z_ORDER = (0, 1, 2, 3, -1, -2, -3, 4)


def pulled(value, axis, steps):
    count = SIZES[axis]
    return lax.ppermute(value, axis, [((i + steps) % count, i) for i in range(count)])


def pulled_z(value, steps):
    def place(z):
        return (z % 2) * SIZES["zh"] + (z % 8) // 2

    return lax.ppermute(value, ("zl", "zh"), [(place((z + steps) % 8), place(z)) for z in range(8)])


def product(left, right):
    return jnp.dot(left, right, precision=lax.Precision.HIGHEST, preferred_element_type=jnp.float32)


def product_nt(left, right):
    return lax.dot_general(
        left,
        right,
        (((1,), (1,)), ((), ())),
        precision=lax.Precision.HIGHEST,
        preferred_element_type=jnp.float32,
    )


def product_tn(left, right):
    return lax.dot_general(
        left,
        right,
        (((0,), (0,)), ((), ())),
        precision=lax.Precision.HIGHEST,
        preferred_element_type=jnp.float32,
    )


def unit_rows(raw):
    scale = lax.rsqrt(jnp.sum(raw * raw, axis=1) + NORM_EPS)
    return (raw * scale[:, None], scale)


def unit_back(unit, scale, grad):
    return scale[:, None] * (grad - unit * jnp.sum(unit * grad, axis=1, keepdims=True))


def gather_plane(rows, first, second):
    line = jnp.concatenate([rows] + [pulled(rows, first, k) for k in (1, 2, 3)])
    return jnp.concatenate([line] + [pulled(line, second, k) for k in (1, 2, 3)])


def scatter_plane(terms, first, second):
    for axis in (second, first):
        size = terms.shape[0] // 4
        terms = sum(
            (pulled(terms[k * size : (k + 1) * size], axis, -k) for k in (1, 2, 3)), terms[:size]
        )
    return terms


def gather_column(rows):
    half = rows.shape[0] // 2
    up, down = pulled_z(rows, 1), pulled_z(rows, -1)
    far_up = pulled_z(jnp.concatenate([rows, up]), 2)
    far_down = pulled_z(jnp.concatenate([rows, down]), -2)
    across = (pulled_z(far_up[2 * half : 3 * half], 1), pulled_z(far_down[3 * half :], -1))
    own = jnp.concatenate([rows, up, far_up, down, far_down, *across])
    return jnp.concatenate([own, pulled(own, "c", 1)])


def scatter_column(terms):
    count = terms.shape[0] // 2
    size = count // 8
    half = size // 2
    terms = terms[:count] + pulled(terms[count:], "c", 1)
    part = {o: terms[k * size : (k + 1) * size] for k, o in enumerate(Z_ORDER)}
    far_up = jnp.concatenate([part[2], part[3][:half] + pulled_z(part[4][:half], -1), part[3][half:]])
    far_down = jnp.concatenate([part[-2], part[-3][:half], part[-3][half:] + pulled_z(part[4][half:], 1)])
    from_down, from_up = pulled_z(far_up, -2), pulled_z(far_down, 2)
    up = part[1] + from_down[size:]
    down = part[-1] + from_up[size:]
    near = part[0] + from_down[:size] + from_up[:size]
    return near + pulled_z(up, -1) + pulled_z(down, 1)


def local(pooled_rows, projection, text_rows, caption_row):
    zl, y, x, c, zh = (lax.axis_index(a) for a in ("zl", "y", "x", "c", "zh"))
    per_shard = pooled_rows.shape[0]
    count = text_rows.shape[0]
    half = count // 2
    captions, caption_scale = unit_rows(text_rows)

    partial = product(pooled_rows, projection)
    parts = [
        lax.dynamic_slice_in_dim(partial, count * ((zh + k) % 4), count, 0) for k in range(4)
    ]
    projected = sum((pulled(parts[k], "zh", -k) for k in (1, 2, 3)), parts[0])
    images, image_scale = unit_rows(projected)

    named = lax.all_gather(
        lax.dynamic_slice_in_dim(caption_row, count * zh, count, 0), ("y", "x"), tiled=False
    ).reshape(4, 4, count)
    named = jnp.roll(jnp.roll(named, -y, axis=0), -x, axis=1)
    named_first = named[:, :, :half].reshape(-1)
    named_second = named[:, :, half:].transpose(1, 0, 2).reshape(-1)

    z = (2 * zh + zl + jnp.array(Z_ORDER, jnp.int32)) % 8
    shard = (((z % 2) * 4 + y) * 4 + x) * 2 + jnp.stack([c, 1 - c])[:, None]
    held = (shard * per_shard + (z // 2) * count)[:, :, None] + jnp.arange(count, dtype=jnp.int32)
    held = held.reshape(-1)

    first = gather_plane(images[:half], "x", "y")
    second = gather_plane(images[half:], "y", "x")
    column = gather_column(captions)

    def weigh(group, group_named):
        logits = LOGIT_SCALE * product_nt(group, column) + LOGIT_BIAS
        signs = jnp.where(group_named[:, None] == held[None, :], 1.0, -1.0).astype(jnp.float32)
        return -signs * jax.nn.sigmoid(-signs * logits)

    weights_first = weigh(first, named_first)
    weights_second = weigh(second, named_second)
    grad_first = scatter_plane(LOGIT_SCALE * product(weights_first, column), "x", "y")
    grad_second = scatter_plane(LOGIT_SCALE * product(weights_second, column), "y", "x")
    column_grad = LOGIT_SCALE * (product_tn(weights_first, first) + product_tn(weights_second, second))

    image_grad = jnp.concatenate([grad_first, grad_second])
    raw_grad = unit_back(images, image_scale, image_grad)
    raw_rows = jnp.concatenate([raw_grad] + [pulled(raw_grad, "zh", k) for k in (1, 2, 3)])
    pooled_grad = jnp.roll(product_nt(raw_rows, projection), count * zh, axis=0)

    caption_grad = scatter_column(column_grad)
    text_grad = unit_back(captions, caption_scale, caption_grad)
    return (pooled_grad, text_grad)


def solution(mesh):
    grid = Mesh(mesh.devices.reshape(tuple(SIZES.values())), tuple(SIZES))
    return jax.shard_map(
        local,
        mesh=grid,
        in_specs=(P(DP, "zh"), P("zh", None), P((*DP, "zh"), None), P(DP)),
        out_specs=(P(DP, "zh"), P((*DP, "zh"), None)),
        check_vma=False,
    )
```

```python
import jax
import jax.numpy as jnp
from jax import lax
from jax.experimental import pallas as pl
from jax.experimental.pallas import tpu as pltpu
from jax.sharding import Mesh, PartitionSpec as P

LOGIT_SCALE = 10.0
LOGIT_BIAS = -2.0
NORM_EPS = 1e-06

SIZES = {"zl": 2, "y": 4, "x": 4, "c": 2, "zh": 4}
DP = ("zl", "y", "x", "c")
COLUMN = ("zl", "zh")
HALF = 16
LINE = 4 * HALF
TAIL = 8


def pulled(value, axis, steps):
    count = SIZES[axis]
    return lax.ppermute(value, axis, [((i + steps) % count, i) for i in range(count)])


def pulls(value, axis):
    return [value] + [pulled(value, axis, k) for k in (1, 2, 3)]


def returned(terms, axis):
    return sum((pulled(terms[k], axis, -k) for k in (1, 2, 3)), terms[0])


def product(left, right, dims):
    return lax.dot_general(
        left,
        right,
        (dims, ((), ())),
        precision=lax.Precision.HIGHEST,
        preferred_element_type=jnp.float32,
    )


def unit_rows(raw):
    scale = lax.rsqrt(jnp.sum(raw * raw, axis=1) + NORM_EPS)
    return (raw * scale[:, None], scale)


def unit_back(unit, scale, grad):
    return scale[:, None] * (grad - unit * jnp.sum(unit * grad, axis=1, keepdims=True))


def parts(value):
    high = value.astype(jnp.bfloat16)
    return high, (value - high.astype(jnp.float32)).astype(jnp.bfloat16)


def dot3(left, right, dims):
    def one(a, b):
        return lax.dot_general(a, b, (dims, ((), ())), preferred_element_type=jnp.float32)

    return one(left[0], right[0]) + (one(left[0], right[1]) + one(left[1], right[0]))


def stack_kernel(a, b, c, d, out):
    for k, ref in enumerate((a, b, c, d)):
        out[k * HALF : (k + 1) * HALF, :] = ref[:HALF, :]
    rows = [ref[HALF : HALF + 1, :] for ref in (a, b, c, d)]
    out[LINE : LINE + TAIL, :] = jnp.concatenate(rows + [jnp.zeros((4, a.shape[1]), jnp.float32)])


def stacked(pieces):
    width = pieces[0].shape[1]
    return pl.pallas_call(
        stack_kernel, out_shape=jax.ShapeDtypeStruct((LINE + TAIL, width), jnp.float32)
    )(*pieces)


def pair_kernel(adds, *refs):
    lines, (own, other, held), refs = refs[:4], refs[4:7], refs[7:]
    before, refs = (refs[:3], refs[3:]) if adds else (None, refs)
    grads, sums = refs[:4], refs[4:6]
    images = parts(jnp.concatenate([r[:LINE, :] for r in lines]))
    captions = parts(jnp.concatenate([own[...], other[...]]))
    if adds:
        wanted = before[2][:, :1]
    else:
        columns = [r[LINE : LINE + TAIL, :128].T for r in lines]

        def spread(pick):
            return jnp.concatenate(
                [jnp.broadcast_to(pick(k, j), (HALF, 128)) for k in range(4) for j in range(4)]
            )

        wanted = spread(lambda k, j: columns[k][:HALF, j : j + 1])[:, :1]
        refs[6][...] = spread(lambda k, j: columns[j][HALF : 2 * HALF, k : k + 1])
    logits = LOGIT_SCALE * dot3(images, captions, ((1,), (1,))) + LOGIT_BIAS
    signs = jnp.where(wanted == held[...], 1.0, -1.0).astype(jnp.float32)
    weights = (-LOGIT_SCALE * signs) * jax.nn.sigmoid(-signs * logits)
    image_terms = dot3(parts(weights), captions, ((1,), (0,)))
    for k, ref in enumerate(grads):
        ref[...] = image_terms[k * LINE : (k + 1) * LINE]
    caption_terms = dot3(parts(weights.T), images, ((1,), (0,)))
    size = own.shape[0]
    for k, ref in enumerate(sums):
        term = caption_terms[k * size : (k + 1) * size]
        ref[...] = term + before[k][...] if adds else term


def pair_terms(lines, captions, held, before):
    rows, width = captions[0].shape
    adds = before is not None
    shapes = [(LINE, width)] * 4 + [(rows, width)] * 2 + ([] if adds else [(4 * LINE, 128)])
    out = pl.pallas_call(
        lambda *refs: pair_kernel(adds, *refs),
        out_shape=[jax.ShapeDtypeStruct(shape, jnp.float32) for shape in shapes],
        compiler_params=pltpu.CompilerParams(vmem_limit_bytes=48 << 20),
        name="pairs",
    )(*lines, *captions, held, *(before or []))
    return out[:4], out[4:]


def scattered(grads, first, second):
    line = returned(grads, second)
    return returned([line[k * HALF : (k + 1) * HALF] for k in range(4)], first)


def local(pooled_rows, projection, text_rows, caption_row):
    zl, y, x, c, zh = (lax.axis_index(a) for a in ("zl", "y", "x", "c", "zh"))
    per_shard = pooled_rows.shape[0]
    count, width = text_rows.shape
    captions, caption_scale = unit_rows(text_rows)

    partial = product(pooled_rows, projection, ((1,), (0,)))
    projected = returned(
        [lax.dynamic_slice_in_dim(partial, count * ((zh + k) % 4), count, 0) for k in range(4)], "zh"
    )
    images, image_scale = unit_rows(projected)

    named = lax.dynamic_slice_in_dim(caption_row, count * zh, count, 0).astype(jnp.float32)
    tail = jnp.pad(named[None, :], ((0, TAIL - 1), (0, width - count)))

    column = lax.all_to_all(jnp.concatenate([captions] * 8), COLUMN, 0, 0, tiled=True)
    across = pulled(column, "c", 1)
    z = jnp.array([0, 2, 4, 6, 1, 3, 5, 7], jnp.int32)
    shard = (((z % 2) * 4 + y) * 4 + x) * 2 + jnp.stack([c, 1 - c])[:, None]
    held = (shard * per_shard + (z // 2) * count)[:, :, None] + jnp.arange(count, dtype=jnp.int32)
    held = held.reshape(1, -1).astype(jnp.float32)

    first = pulls(stacked(pulls(jnp.concatenate([images[:HALF], tail]), "x")), "y")
    second = pulls(jnp.concatenate(pulls(images[HALF:], "y")), "x")

    grads_first, sums = pair_terms(first, (column, across), held, None)
    grads_second, sums = pair_terms(second, (column, across), held, sums)

    column_sum = sums[0] + pulled(sums[1], "c", 1)
    caption_terms = lax.all_to_all(column_sum, COLUMN, 0, 0, tiled=True)
    caption_grad = jnp.sum(caption_terms.reshape(8, count, width), axis=0)
    text_grad = unit_back(captions, caption_scale, caption_grad)

    image_grad = jnp.concatenate(
        [scattered(grads_first, "x", "y"), scattered(grads_second, "y", "x")]
    )
    raw_grad = unit_back(images, image_scale, image_grad)
    raw_rows = jnp.concatenate(pulls(raw_grad, "zh"))
    pooled_grad = jnp.roll(product(raw_rows, projection, ((1,), (1,))), count * zh, axis=0)
    return (pooled_grad, text_grad)


def solution(mesh):
    grid = Mesh(mesh.devices.reshape(tuple(SIZES.values())), tuple(SIZES))
    return jax.shard_map(
        local,
        mesh=grid,
        in_specs=(P(DP, "zh"), P("zh", None), P((*DP, "zh"), None), P(DP)),
        out_specs=(P(DP, "zh"), P((*DP, "zh"), None)),
        check_vma=False,
    )
```

```python
import jax
import jax.numpy as jnp
from jax import lax
from jax.experimental import pallas as pl
from jax.experimental.pallas import tpu as pltpu
from jax.sharding import Mesh, PartitionSpec as P

LOGIT_SCALE = 10.0
LOGIT_BIAS = -2.0
NORM_EPS = 1e-06

SIZES = {"zl": 2, "y": 4, "x": 4, "c": 2, "zh": 4}
DP = ("zl", "y", "x", "c")


def pulled(value, axis, steps):
    count = SIZES[axis]
    return lax.ppermute(value, axis, [((i + steps) % count, i) for i in range(count)])


def pulls(value, axis):
    return [value] + [pulled(value, axis, k) for k in (1, 2, 3)]


def returned(terms, axis):
    return sum((pulled(terms[k], axis, -k) for k in (1, 2, 3)), terms[0])


def product(left, right, dims):
    return lax.dot_general(
        left,
        right,
        (dims, ((), ())),
        precision=lax.Precision.HIGHEST,
        preferred_element_type=jnp.float32,
    )


def unit_rows(raw):
    scale = lax.rsqrt(jnp.sum(raw * raw, axis=1) + NORM_EPS)
    return (raw * scale[:, None], scale)


def unit_back(unit, scale, grad):
    return scale[:, None] * (grad - unit * jnp.sum(unit * grad, axis=1, keepdims=True))


def parts(value):
    high = value.astype(jnp.bfloat16)
    return high, (value - high.astype(jnp.float32)).astype(jnp.bfloat16)


def dot3(left, right, dims):
    def one(a, b):
        return lax.dot_general(a, b, (dims, ((), ())), preferred_element_type=jnp.float32)

    return one(left[0], right[0]) + (one(left[0], right[1]) + one(left[1], right[0]))


def image_kernel(adds, *refs):
    own, other, wanted, held = refs[:4]
    blocks, refs = refs[4:8], refs[8:]
    before, refs = (refs[:2], refs[2:]) if adds else (None, refs)
    grads, weights_out = refs[:2], refs[2]
    images = parts(jnp.concatenate([own[...], other[...]]))
    captions = parts(jnp.concatenate([r[...] for r in blocks]))
    logits = LOGIT_SCALE * dot3(images, captions, ((1,), (1,))) + LOGIT_BIAS
    signs = jnp.where(wanted[:, :1] == held[...], 1.0, -1.0).astype(jnp.float32)
    weights = (-LOGIT_SCALE * signs) * jax.nn.sigmoid(-signs * logits)
    weights_out[...] = weights
    image_terms = dot3(parts(weights), captions, ((1,), (0,)))
    size = own.shape[0]
    for k, ref in enumerate(grads):
        term = image_terms[k * size : (k + 1) * size]
        ref[...] = term + before[k][...] if adds else term


def caption_kernel(own, other, weights, *sums):
    images = parts(jnp.concatenate([own[...], other[...]]))
    caption_terms = dot3(parts(weights[...].T), images, ((1,), (0,)))
    size = sums[0].shape[0]
    for k, ref in enumerate(sums):
        ref[...] = caption_terms[k * size : (k + 1) * size]


def called(kernel, name, shapes, *args):
    return pl.pallas_call(
        kernel,
        out_shape=[jax.ShapeDtypeStruct(shape, jnp.float32) for shape in shapes],
        compiler_params=pltpu.CompilerParams(vmem_limit_bytes=48 << 20),
        name=name,
    )(*args)


def image_terms(images, wanted, held, blocks, before):
    shapes = [images[0].shape] * 2 + [(wanted.shape[0], held.shape[1])]
    out = called(
        lambda *refs: image_kernel(before is not None, *refs),
        "image_terms", shapes, *images, wanted, held, *blocks, *(before or []),
    )
    return out[:2], out[2]


def caption_terms(images, weights, shape):
    return called(caption_kernel, "caption_terms", [shape] * 4, *images, weights)


def shared(rows):
    rows = jnp.broadcast_to(rows[None], (4, *rows.shape)).reshape(-1, rows.shape[1])
    return lax.all_to_all(rows, "zh", 0, 0, tiled=True)


def line_parts(line):
    size = line.shape[0] // 4
    return [line[k * size : (k + 1) * size] for k in range(4)]


def local(pooled_rows, projection, text_rows, caption_row):
    zl, y, x, c, zh = (lax.axis_index(a) for a in ("zl", "y", "x", "c", "zh"))
    per_shard = pooled_rows.shape[0]
    count, width = text_rows.shape
    captions, caption_scale = unit_rows(text_rows)

    partial = product(pooled_rows, projection, ((1,), (0,)))
    partial, moved = lax.optimization_barrier((partial, pulled(captions, "zl", 1)))
    projected = jnp.sum(
        lax.all_to_all(partial, "zh", 0, 0, tiled=True).reshape(4, count, width), axis=0
    )

    near_line = jnp.concatenate(pulls(captions, "x"))
    far_line = jnp.concatenate(pulls(moved, "y"))
    near_line, far_line, projected = lax.optimization_barrier((near_line, far_line, projected))
    near = pulls(near_line, "y")
    far = pulls(far_line, "x")
    images, image_scale = unit_rows(projected)
    shard_images = shared(images)
    chip_images = [shard_images, pulled(shard_images, "c", 1)]

    named = caption_row.astype(jnp.float32)
    wanted = jnp.concatenate([named, pulled(named, "c", 1)])
    wanted = jnp.broadcast_to(wanted[:, None], (2 * per_shard, 128))

    steps = jnp.arange(4, dtype=jnp.int32)
    rows = jnp.arange(count, dtype=jnp.int32)

    def numbers(zl, y, x):
        shard = ((zl * 4 + y % 4) * 4 + x % 4) * 2 + c
        held = (shard * per_shard + zh * count)[:, :, None] + rows
        return held.reshape(1, -1).astype(jnp.float32)

    near_held = numbers(zl, (y + steps)[:, None], (x + steps)[None, :])
    far_held = numbers(1 - zl, (y + steps)[None, :], (x + steps)[:, None])

    grads, near_weights = image_terms(chip_images, wanted, near_held, near, None)
    grads, far_weights = image_terms(chip_images, wanted, far_held, far, grads)
    grads, near_weights = lax.optimization_barrier((grads, near_weights))
    near_sums = caption_terms(chip_images, near_weights, near[0].shape)
    shard_grad = grads[0] + pulled(grads[1], "c", 1)
    shard_grad, far_weights = lax.optimization_barrier((shard_grad, far_weights))
    far_sums = caption_terms(chip_images, far_weights, far[0].shape)

    image_grad = jnp.sum(
        lax.all_to_all(shard_grad, "zh", 0, 0, tiled=True).reshape(4, count, width), axis=0
    )
    near_line = returned(near_sums, "y")
    far_line = returned(far_sums, "x")
    near_line, far_line, image_grad = lax.optimization_barrier((near_line, far_line, image_grad))
    far_sum = returned(line_parts(far_line), "y")
    caption_grad = returned(line_parts(near_line), "x") + pulled(far_sum, "zl", 1)
    raw_grad = unit_back(images, image_scale, image_grad)
    pooled_grad = product(shared(raw_grad), projection, ((1,), (1,)))

    text_grad = unit_back(captions, caption_scale, caption_grad)
    return (pooled_grad, text_grad)


def solution(mesh):
    grid = Mesh(mesh.devices.reshape(tuple(SIZES.values())), tuple(SIZES))
    return jax.shard_map(
        local,
        mesh=grid,
        in_specs=(P(DP, "zh"), P("zh", None), P((*DP, "zh"), None), P(DP)),
        out_specs=(P(DP, "zh"), P((*DP, "zh"), None)),
        check_vma=False,
    )
```

```python
import jax
import jax.numpy as jnp
from jax import lax
from jax.experimental import pallas as pl
from jax.experimental.pallas import tpu as pltpu
from jax.sharding import Mesh, PartitionSpec as P

LOGIT_SCALE = 10.0
LOGIT_BIAS = -2.0
NORM_EPS = 1e-06

SIZES = {"zl": 2, "y": 4, "x": 4, "c": 2, "zh": 4}
DP = ("zl", "y", "x", "c")
LONG = pl.CostEstimate(flops=30_000_000_000, transcendentals=0, bytes_accessed=100_000_000)


def pulled(value, axis, steps):
    count = SIZES[axis]
    return lax.ppermute(value, axis, [((i + steps) % count, i) for i in range(count)])


def pulls(value, axis):
    return [value] + [pulled(value, axis, k) for k in (1, 2, 3)]


def returned(terms, axis):
    return sum((pulled(terms[k], axis, -k) for k in (1, 2, 3)), terms[0])


def product(left, right, dims):
    return lax.dot_general(
        left,
        right,
        (dims, ((), ())),
        precision=lax.Precision.HIGHEST,
        preferred_element_type=jnp.float32,
    )


def unit_back(unit, scale, grad):
    return scale[:, None] * (grad - unit * jnp.sum(unit * grad, axis=1, keepdims=True))


def parts(value):
    high = value.astype(jnp.bfloat16)
    return high, (value - high.astype(jnp.float32)).astype(jnp.bfloat16)


def dot3(left, right, dims):
    def one(a, b):
        return lax.dot_general(a, b, (dims, ((), ())), preferred_element_type=jnp.float32)

    return one(left[0], right[0]) + (one(left[0], right[1]) + one(left[1], right[0]))


def image_kernel(adds, *refs):
    own, other, wanted, held = refs[:4]
    blocks, refs = refs[4:8], refs[8:]
    before, refs = (refs[:2], refs[2:]) if adds else (None, refs)
    grads, weights_out = refs[:2], refs[2]
    images = parts(jnp.concatenate([own[...], other[...]]))
    captions = parts(jnp.concatenate([r[...] for r in blocks]))
    logits = LOGIT_SCALE * dot3(images, captions, ((1,), (1,))) + LOGIT_BIAS
    signs = jnp.where(wanted[:, :1] == held[...], 1.0, -1.0).astype(jnp.float32)
    weights = (-LOGIT_SCALE * signs) * jax.nn.sigmoid(-signs * logits)
    weights_out[...] = weights
    image_terms = dot3(parts(weights), captions, ((1,), (0,)))
    size = own.shape[0]
    for k, ref in enumerate(grads):
        term = image_terms[k * size : (k + 1) * size]
        ref[...] = term + before[k][...] if adds else term


def caption_kernel(own, other, weights, *sums):
    images = parts(jnp.concatenate([own[...], other[...]]))
    caption_terms = dot3(parts(weights[...].T), images, ((1,), (0,)))
    size = sums[0].shape[0]
    for k, ref in enumerate(sums):
        ref[...] = caption_terms[k * size : (k + 1) * size]


def called(kernel, name, shapes, *args, cost=None):
    return pl.pallas_call(
        kernel,
        out_shape=[jax.ShapeDtypeStruct(shape, jnp.float32) for shape in shapes],
        compiler_params=pltpu.CompilerParams(vmem_limit_bytes=48 << 20),
        name=name,
        cost_estimate=cost,
    )(*args)


def image_terms(images, wanted, held, blocks, before):
    shapes = [images[0].shape] * 2 + [(wanted.shape[0], held.shape[1])]
    out = called(
        lambda *refs: image_kernel(before is not None, *refs),
        "image_terms", shapes, *images, wanted, held, *blocks, *(before or []),
    )
    return out[:2], out[2]


def caption_terms(images, weights, shape, cost=None):
    return called(caption_kernel, "caption_terms", [shape] * 4, *images, weights, cost=cost)


def sum_kernel(a, b, c, d, out):
    out[...] = (a[...] + b[...]) + (c[...] + d[...])


def summed(parts, cost=None):
    return called(sum_kernel, "line_sum", [parts[0].shape], *parts, cost=cost)[0]


def unit_kernel(raw, unit, scale):
    rows = raw[...]
    factor = lax.rsqrt(jnp.sum(rows * rows, axis=1, keepdims=True) + NORM_EPS)
    unit[...] = rows * factor
    scale[...] = jnp.broadcast_to(factor, scale.shape)


def image_unit_kernel(raw, unit, scale, sent):
    size = unit.shape[0]
    rows = sum(raw[k * size : (k + 1) * size] for k in range(4))
    factor = lax.rsqrt(jnp.sum(rows * rows, axis=1, keepdims=True) + NORM_EPS)
    unit[...] = rows * factor
    scale[...] = jnp.broadcast_to(factor, scale.shape)
    for k in range(4):
        sent[k * size : (k + 1) * size] = rows * factor


def raw_kernel(terms, unit, scale, sent):
    size = unit.shape[0]
    grad = sum(terms[k * size : (k + 1) * size] for k in range(4))
    dot = jnp.sum(unit[...] * grad, axis=1, keepdims=True)
    raw = scale[:, :1] * (grad - unit[...] * dot)
    for k in range(4):
        sent[k * size : (k + 1) * size] = raw


def line_parts(line):
    size = line.shape[0] // 4
    return [line[k * size : (k + 1) * size] for k in range(4)]


def local(pooled_rows, projection, text_rows, caption_row):
    zl, y, x, c, zh = (lax.axis_index(a) for a in ("zl", "y", "x", "c", "zh"))
    per_shard = pooled_rows.shape[0]
    count, width = text_rows.shape
    captions, caption_scale = called(
        unit_kernel, "caption_rows", [(count, width), (count, 128)], text_rows
    )

    partial = product(pooled_rows, projection, ((1,), (0,)))
    partial, moved = lax.optimization_barrier((partial, pulled(captions, "zl", 1)))
    arrived = lax.all_to_all(partial, "zh", 0, 0, tiled=True)

    near_line = jnp.concatenate(pulls(captions, "x"))
    far_line = jnp.concatenate(pulls(moved, "y"))
    near_line, far_line, arrived = lax.optimization_barrier((near_line, far_line, arrived))
    near = pulls(near_line, "y")
    far = pulls(far_line, "x")
    images, image_scale, sent = called(
        image_unit_kernel, "image_rows", [(count, width), (count, 128), partial.shape], arrived
    )
    shard_images = lax.all_to_all(sent, "zh", 0, 0, tiled=True)
    chip_images = [shard_images, pulled(shard_images, "c", 1)]

    named = caption_row.astype(jnp.float32)
    wanted = jnp.concatenate([named, pulled(named, "c", 1)])
    wanted = jnp.broadcast_to(wanted[:, None], (2 * per_shard, 128))

    steps = jnp.arange(4, dtype=jnp.int32)
    rows = jnp.arange(count, dtype=jnp.int32)

    def numbers(zl, y, x):
        shard = ((zl * 4 + y % 4) * 4 + x % 4) * 2 + c
        held = (shard * per_shard + zh * count)[:, :, None] + rows
        return held.reshape(1, -1).astype(jnp.float32)

    near_held = numbers(zl, (y + steps)[:, None], (x + steps)[None, :])
    far_held = numbers(1 - zl, (y + steps)[None, :], (x + steps)[:, None])

    grads, near_weights = image_terms(chip_images, wanted, near_held, near, None)
    grads, far_weights = image_terms(chip_images, wanted, far_held, far, grads)
    grads, far_weights = lax.optimization_barrier((grads, far_weights))
    far_sums = caption_terms(chip_images, far_weights, far[0].shape)
    shard_grad = grads[0] + pulled(grads[1], "c", 1)
    shard_grad, near_weights = lax.optimization_barrier((shard_grad, near_weights))
    near_sums = caption_terms(chip_images, near_weights, near[0].shape, cost=LONG)

    (sent,) = called(
        raw_kernel,
        "image_back",
        [shard_grad.shape],
        lax.all_to_all(shard_grad, "zh", 0, 0, tiled=True),
        images,
        image_scale,
    )
    near_parts = [near_sums[0]] + [pulled(near_sums[k], "y", -k) for k in (1, 2, 3)]
    far_parts = [far_sums[0]] + [pulled(far_sums[k], "x", -k) for k in (1, 2, 3)]
    raw_rows = lax.all_to_all(sent, "zh", 0, 0, tiled=True)

    far_parts, sent = lax.optimization_barrier((far_parts, sent))
    far_line = summed(far_parts, cost=LONG)
    near_parts, _ = lax.optimization_barrier((near_parts, far_line))
    far_own, *far_rest = line_parts(far_line)
    far_rest = [pulled(part, "y", -k) for k, part in enumerate(far_rest, 1)]
    far_own, raw_rows = lax.optimization_barrier((far_own, raw_rows))
    pooled_grad = product(raw_rows, projection, ((1,), (1,)))
    far_sum = sum(far_rest, far_own)
    near_sum = returned(line_parts(summed(near_parts)), "x")
    caption_grad = near_sum + pulled(far_sum, "zl", 1)
    text_grad = unit_back(captions, caption_scale[:, 0], caption_grad)
    return (pooled_grad, text_grad)


def solution(mesh):
    grid = Mesh(mesh.devices.reshape(tuple(SIZES.values())), tuple(SIZES))
    return jax.shard_map(
        local,
        mesh=grid,
        in_specs=(P(DP, "zh"), P("zh", None), P((*DP, "zh"), None), P(DP)),
        out_specs=(P(DP, "zh"), P((*DP, "zh"), None)),
        check_vma=False,
    )
```

```python
import jax
import jax.numpy as jnp
from jax import lax
from jax.experimental import pallas as pl
from jax.experimental.pallas import tpu as pltpu
from jax.sharding import Mesh, PartitionSpec as P

LOGIT_SCALE = 10.0
LOGIT_BIAS = -2.0
NORM_EPS = 1e-06

SIZES = {"zl": 2, "y": 4, "x": 4, "c": 2, "zh": 4}
DP = ("zl", "y", "x", "c")
LONG = pl.CostEstimate(flops=30_000_000_000, transcendentals=0, bytes_accessed=100_000_000)


def pulled(value, axis, steps):
    count = SIZES[axis]
    return lax.ppermute(value, axis, [((i + steps) % count, i) for i in range(count)])


def pulls(value, axis):
    return [value] + [pulled(value, axis, k) for k in (1, 2, 3)]


def returned(terms, axis):
    return sum((pulled(terms[k], axis, -k) for k in (1, 2, 3)), terms[0])


def product(left, right, dims):
    return lax.dot_general(
        left,
        right,
        (dims, ((), ())),
        precision=lax.Precision.HIGHEST,
        preferred_element_type=jnp.float32,
    )


def unit_back(unit, scale, grad):
    return scale[:, None] * (grad - unit * jnp.sum(unit * grad, axis=1, keepdims=True))


def parts(value):
    high = value.astype(jnp.bfloat16)
    return high, (value - high.astype(jnp.float32)).astype(jnp.bfloat16)


def dot3(left, right, dims):
    def one(a, b):
        return lax.dot_general(a, b, (dims, ((), ())), preferred_element_type=jnp.float32)

    return one(left[0], right[0]) + (one(left[0], right[1]) + one(left[1], right[0]))


def image_kernel(own, other, wanted, held, *refs):
    blocks, grads, weights_out = refs[:8], refs[8:10], refs[10:]
    images = parts(jnp.concatenate([own[...], other[...]]))
    terms = 0.0
    for h, out in enumerate(weights_out):
        captions = parts(jnp.concatenate([r[...] for r in blocks[4 * h : 4 * h + 4]]))
        logits = LOGIT_SCALE * dot3(images, captions, ((1,), (1,))) + LOGIT_BIAS
        signs = jnp.where(wanted[:, :1] == held[h : h + 1, :], 1.0, -1.0).astype(jnp.float32)
        weights = (-LOGIT_SCALE * signs) * jax.nn.sigmoid(-signs * logits)
        out[...] = weights
        terms = terms + dot3(parts(weights), captions, ((1,), (0,)))
    size = own.shape[0]
    for k, ref in enumerate(grads):
        ref[...] = terms[k * size : (k + 1) * size]


def caption_kernel(own, other, weights, *sums):
    images = parts(jnp.concatenate([own[...], other[...]]))
    caption_terms = dot3(parts(weights[...].T), images, ((1,), (0,)))
    size = sums[0].shape[0]
    for k, ref in enumerate(sums):
        ref[...] = caption_terms[k * size : (k + 1) * size]


def called(kernel, name, shapes, *args, cost=None):
    return pl.pallas_call(
        kernel,
        out_shape=[jax.ShapeDtypeStruct(shape, jnp.float32) for shape in shapes],
        compiler_params=pltpu.CompilerParams(vmem_limit_bytes=48 << 20),
        name=name,
        cost_estimate=cost,
    )(*args)


def image_terms(images, wanted, held, blocks):
    shapes = [images[0].shape] * 2 + [(wanted.shape[0], held.shape[1])] * 2
    out = called(image_kernel, "image_terms", shapes, *images, wanted, held, *blocks)
    return out[:2], out[2], out[3]


def caption_terms(images, weights, shape, cost=None):
    return called(caption_kernel, "caption_terms", [shape] * 4, *images, weights, cost=cost)


def sum_kernel(a, b, c, d, out):
    out[...] = (a[...] + b[...]) + (c[...] + d[...])


def summed(parts, cost=None):
    return called(sum_kernel, "line_sum", [parts[0].shape], *parts, cost=cost)[0]


def unit_kernel(raw, unit, scale):
    rows = raw[...]
    factor = lax.rsqrt(jnp.sum(rows * rows, axis=1, keepdims=True) + NORM_EPS)
    unit[...] = rows * factor
    scale[...] = jnp.broadcast_to(factor, scale.shape)


def image_unit_kernel(raw, unit, scale, sent):
    size = unit.shape[0]
    rows = sum(raw[k * size : (k + 1) * size] for k in range(4))
    factor = lax.rsqrt(jnp.sum(rows * rows, axis=1, keepdims=True) + NORM_EPS)
    unit[...] = rows * factor
    scale[...] = jnp.broadcast_to(factor, scale.shape)
    for k in range(4):
        sent[k * size : (k + 1) * size] = rows * factor


def raw_kernel(terms, unit, scale, sent):
    size = unit.shape[0]
    grad = sum(terms[k * size : (k + 1) * size] for k in range(4))
    dot = jnp.sum(unit[...] * grad, axis=1, keepdims=True)
    raw = scale[:, :1] * (grad - unit[...] * dot)
    for k in range(4):
        sent[k * size : (k + 1) * size] = raw


def line_parts(line):
    size = line.shape[0] // 4
    return [line[k * size : (k + 1) * size] for k in range(4)]


def local(pooled_rows, projection, text_rows, caption_row):
    zl, y, x, c, zh = (lax.axis_index(a) for a in ("zl", "y", "x", "c", "zh"))
    per_shard = pooled_rows.shape[0]
    count, width = text_rows.shape
    captions, caption_scale = called(
        unit_kernel, "caption_rows", [(count, width), (count, 128)], text_rows
    )

    partial = product(pooled_rows, projection, ((1,), (0,)))
    partial, moved = lax.optimization_barrier((partial, pulled(captions, "zl", 1)))
    arrived = lax.all_to_all(partial, "zh", 0, 0, tiled=True)

    near_line = jnp.concatenate(pulls(captions, "x"))
    far_line = jnp.concatenate(pulls(moved, "y"))
    near_line, far_line, arrived = lax.optimization_barrier((near_line, far_line, arrived))
    near = pulls(near_line, "y")
    far = pulls(far_line, "x")
    images, image_scale, sent = called(
        image_unit_kernel, "image_rows", [(count, width), (count, 128), partial.shape], arrived
    )
    shard_images = lax.all_to_all(sent, "zh", 0, 0, tiled=True)
    chip_images = [shard_images, pulled(shard_images, "c", 1)]

    named = caption_row.astype(jnp.float32)
    wanted = jnp.concatenate([named, pulled(named, "c", 1)])
    wanted = jnp.broadcast_to(wanted[:, None], (2 * per_shard, 128))

    steps = jnp.arange(4, dtype=jnp.int32)
    rows = jnp.arange(count, dtype=jnp.int32)

    def numbers(zl, y, x):
        shard = ((zl * 4 + y % 4) * 4 + x % 4) * 2 + c
        held = (shard * per_shard + zh * count)[:, :, None] + rows
        return held.reshape(1, -1).astype(jnp.float32)

    near_held = numbers(zl, (y + steps)[:, None], (x + steps)[None, :])
    far_held = numbers(1 - zl, (y + steps)[None, :], (x + steps)[:, None])

    held = jnp.concatenate([near_held, far_held])
    grads, near_weights, far_weights = image_terms(chip_images, wanted, held, [*near, *far])
    grads, far_weights = lax.optimization_barrier((grads, far_weights))
    far_sums = caption_terms(chip_images, far_weights, far[0].shape)
    shard_grad = grads[0] + pulled(grads[1], "c", 1)
    shard_grad, near_weights = lax.optimization_barrier((shard_grad, near_weights))
    near_sums = caption_terms(chip_images, near_weights, near[0].shape, cost=LONG)

    (sent,) = called(
        raw_kernel,
        "image_back",
        [shard_grad.shape],
        lax.all_to_all(shard_grad, "zh", 0, 0, tiled=True),
        images,
        image_scale,
    )
    near_parts = [near_sums[0]] + [pulled(near_sums[k], "y", -k) for k in (1, 2, 3)]
    far_parts = [far_sums[0]] + [pulled(far_sums[k], "x", -k) for k in (1, 2, 3)]
    raw_rows = lax.all_to_all(sent, "zh", 0, 0, tiled=True)

    far_parts, sent = lax.optimization_barrier((far_parts, sent))
    far_line = summed(far_parts, cost=LONG)
    near_parts, _ = lax.optimization_barrier((near_parts, far_line))
    far_own, *far_rest = line_parts(far_line)
    far_rest = [pulled(part, "y", -k) for k, part in enumerate(far_rest, 1)]
    far_own, raw_rows = lax.optimization_barrier((far_own, raw_rows))
    pooled_grad = product(raw_rows, projection, ((1,), (1,)))
    far_sum = sum(far_rest, far_own)
    near_sum = returned(line_parts(summed(near_parts)), "x")
    caption_grad = near_sum + pulled(far_sum, "zl", 1)
    text_grad = unit_back(captions, caption_scale[:, 0], caption_grad)
    return (pooled_grad, text_grad)


def solution(mesh):
    grid = Mesh(mesh.devices.reshape(tuple(SIZES.values())), tuple(SIZES))
    return jax.shard_map(
        local,
        mesh=grid,
        in_specs=(P(DP, "zh"), P("zh", None), P((*DP, "zh"), None), P(DP)),
        out_specs=(P(DP, "zh"), P((*DP, "zh"), None)),
        check_vma=False,
    )
```

```python
import jax
import jax.numpy as jnp
from jax import lax
from jax.experimental import pallas as pl
from jax.experimental.pallas import tpu as pltpu
from jax.sharding import Mesh, PartitionSpec as P

LOGIT_SCALE = 10.0
LOGIT_BIAS = -2.0
NORM_EPS = 1e-06

SIZES = {"zl": 2, "y": 4, "x": 4, "c": 2, "zh": 4}
DP = ("zl", "y", "x", "c")
LONG = pl.CostEstimate(flops=30_000_000_000, transcendentals=0, bytes_accessed=100_000_000)


def pulled(value, axis, steps):
    count = SIZES[axis]
    return lax.ppermute(value, axis, [((i + steps) % count, i) for i in range(count)])


def pulls(value, axis):
    return [value] + [pulled(value, axis, k) for k in (1, 2, 3)]


def ring(value, axis):
    half = value.shape[0] // 2
    up, down = pulled(value, axis, 1), pulled(value, axis, -1)
    return [value, up, pulled(up[:half], axis, 1), pulled(down[half:], axis, -1), down]


def returned(terms, axis):
    return sum((pulled(terms[k], axis, -k) for k in (1, 2, 3)), terms[0])


def product(left, right, dims):
    return lax.dot_general(
        left,
        right,
        (dims, ((), ())),
        precision=lax.Precision.HIGHEST,
        preferred_element_type=jnp.float32,
    )


def unit_back(unit, scale, grad):
    return scale[:, None] * (grad - unit * jnp.sum(unit * grad, axis=1, keepdims=True))


def parts(value):
    high = value.astype(jnp.bfloat16)
    return high, (value - high.astype(jnp.float32)).astype(jnp.bfloat16)


def dot3(left, right, dims):
    def one(a, b):
        return lax.dot_general(a, b, (dims, ((), ())), preferred_element_type=jnp.float32)

    return one(left[0], right[0]) + (one(left[0], right[1]) + one(left[1], right[0]))


def image_kernel(own, other, wanted, held, *refs):
    blocks, grads, weights_out = refs[:10], refs[10:12], refs[12:]
    images = parts(jnp.concatenate([own[...], other[...]]))
    terms = 0.0
    for h, out in enumerate(weights_out):
        captions = parts(jnp.concatenate([r[...] for r in blocks[5 * h : 5 * h + 5]]))
        logits = LOGIT_SCALE * dot3(images, captions, ((1,), (1,))) + LOGIT_BIAS
        signs = jnp.where(wanted[:, :1] == held[h : h + 1, :], 1.0, -1.0).astype(jnp.float32)
        weights = (-LOGIT_SCALE * signs) * jax.nn.sigmoid(-signs * logits)
        out[...] = weights
        terms = terms + dot3(parts(weights), captions, ((1,), (0,)))
    size = own.shape[0]
    for k, ref in enumerate(grads):
        ref[...] = terms[k * size : (k + 1) * size]


def caption_kernel(own, other, weights, *sums):
    images = parts(jnp.concatenate([own[...], other[...]]))
    caption_terms = dot3(parts(weights[...].T), images, ((1,), (0,)))
    start = 0
    for ref in sums:
        ref[...] = caption_terms[start : start + ref.shape[0]]
        start += ref.shape[0]


def called(kernel, name, shapes, *args, cost=None):
    return pl.pallas_call(
        kernel,
        out_shape=[jax.ShapeDtypeStruct(shape, jnp.float32) for shape in shapes],
        compiler_params=pltpu.CompilerParams(vmem_limit_bytes=48 << 20),
        name=name,
        cost_estimate=cost,
    )(*args)


def image_terms(images, wanted, held, blocks):
    shapes = [images[0].shape] * 2 + [(wanted.shape[0], held.shape[1])] * 2
    out = called(image_kernel, "image_terms", shapes, *images, wanted, held, *blocks)
    return out[:2], out[2], out[3]


def caption_terms(images, weights, blocks, cost=None):
    shapes = [blocks[0].shape] * 4
    return called(caption_kernel, "caption_terms", shapes, *images, weights, cost=cost)


def sum_kernel(a, b, c, d, out):
    out[...] = (a[...] + b[...]) + (c[...] + d[...])


def summed(parts, cost=None):
    return called(sum_kernel, "line_sum", [parts[0].shape], *parts, cost=cost)[0]


def unit_kernel(raw, unit, scale):
    rows = raw[...]
    factor = lax.rsqrt(jnp.sum(rows * rows, axis=1, keepdims=True) + NORM_EPS)
    unit[...] = rows * factor
    scale[...] = jnp.broadcast_to(factor, scale.shape)


def image_unit_kernel(raw, unit, scale, sent):
    size = unit.shape[0]
    rows = sum(raw[k * size : (k + 1) * size] for k in range(4))
    factor = lax.rsqrt(jnp.sum(rows * rows, axis=1, keepdims=True) + NORM_EPS)
    unit[...] = rows * factor
    scale[...] = jnp.broadcast_to(factor, scale.shape)
    for k in range(4):
        sent[k * size : (k + 1) * size] = rows * factor


def raw_kernel(terms, unit, scale, sent):
    size = unit.shape[0]
    grad = sum(terms[k * size : (k + 1) * size] for k in range(4))
    dot = jnp.sum(unit[...] * grad, axis=1, keepdims=True)
    raw = scale[:, :1] * (grad - unit[...] * dot)
    for k in range(4):
        sent[k * size : (k + 1) * size] = raw


def line_parts(line):
    size = line.shape[0] // 4
    return [line[k * size : (k + 1) * size] for k in range(4)]


def local(pooled_rows, projection, text_rows, caption_row):
    zl, y, x, c, zh = (lax.axis_index(a) for a in ("zl", "y", "x", "c", "zh"))
    per_shard = pooled_rows.shape[0]
    count, width = text_rows.shape
    captions, caption_scale = called(
        unit_kernel, "caption_rows", [(count, width), (count, 128)], text_rows
    )

    partial = product(pooled_rows, projection, ((1,), (0,)))
    partial, moved = lax.optimization_barrier((partial, pulled(captions, "zl", 1)))
    arrived = lax.all_to_all(partial, "zh", 0, 0, tiled=True)

    near_line = jnp.concatenate(pulls(captions, "x"))
    far_line = jnp.concatenate(pulls(moved, "y"))
    near_line, far_line, arrived = lax.optimization_barrier((near_line, far_line, arrived))
    near = ring(near_line, "y")
    far = ring(far_line, "x")
    images, image_scale, sent = called(
        image_unit_kernel, "image_rows", [(count, width), (count, 128), partial.shape], arrived
    )
    shard_images = lax.all_to_all(sent, "zh", 0, 0, tiled=True)
    chip_images = [shard_images, pulled(shard_images, "c", 1)]

    named = caption_row.astype(jnp.float32)
    wanted = jnp.concatenate([named, pulled(named, "c", 1)])
    wanted = jnp.broadcast_to(wanted[:, None], (2 * per_shard, 128))

    steps = jnp.arange(4, dtype=jnp.int32)
    rows = jnp.arange(count, dtype=jnp.int32)

    def numbers(zl, y, x):
        shard = ((zl * 4 + y % 4) * 4 + x % 4) * 2 + c
        held = (shard * per_shard + zh * count)[:, :, None] + rows
        return held.reshape(1, -1).astype(jnp.float32)

    near_held = numbers(zl, (y + steps)[:, None], (x + steps)[None, :])
    far_held = numbers(1 - zl, (y + steps)[None, :], (x + steps)[:, None])

    held = jnp.concatenate([near_held, far_held])
    grads, near_weights, far_weights = image_terms(chip_images, wanted, held, [*near, *far])
    grads, far_weights = lax.optimization_barrier((grads, far_weights))
    far_sums = caption_terms(chip_images, far_weights, far, cost=LONG)
    shard_grad = grads[0] + pulled(grads[1], "c", 1)
    shard_grad, near_weights = lax.optimization_barrier((shard_grad, near_weights))
    near_sums = caption_terms(chip_images, near_weights, near, cost=LONG)

    (sent,) = called(
        raw_kernel,
        "image_back",
        [shard_grad.shape],
        lax.all_to_all(shard_grad, "zh", 0, 0, tiled=True),
        images,
        image_scale,
    )
    near_parts = [near_sums[0]] + [pulled(near_sums[k], "y", -k) for k in (1, 2, 3)]
    far_parts = [far_sums[0]] + [pulled(far_sums[k], "x", -k) for k in (1, 2, 3)]
    raw_rows = lax.all_to_all(sent, "zh", 0, 0, tiled=True)

    far_parts, sent = lax.optimization_barrier((far_parts, sent))
    far_line = summed(far_parts, cost=LONG)
    near_parts, _ = lax.optimization_barrier((near_parts, far_line))
    far_own, *far_rest = line_parts(far_line)
    far_rest = [pulled(part, "y", -k) for k, part in enumerate(far_rest, 1)]
    far_own, raw_rows = lax.optimization_barrier((far_own, raw_rows))
    pooled_grad = product(raw_rows, projection, ((1,), (1,)))
    far_sum = sum(far_rest, far_own)
    near_sum = returned(line_parts(summed(near_parts)), "x")
    caption_grad = near_sum + pulled(far_sum, "zl", 1)
    text_grad = unit_back(captions, caption_scale[:, 0], caption_grad)
    return (pooled_grad, text_grad)


def solution(mesh):
    grid = Mesh(mesh.devices.reshape(tuple(SIZES.values())), tuple(SIZES))
    return jax.shard_map(
        local,
        mesh=grid,
        in_specs=(P(DP, "zh"), P("zh", None), P((*DP, "zh"), None), P(DP)),
        out_specs=(P(DP, "zh"), P((*DP, "zh"), None)),
        check_vma=False,
    )
```

```python
import jax
import jax.numpy as jnp
from jax import lax
from jax.experimental import pallas as pl
from jax.experimental.pallas import tpu as pltpu
from jax.sharding import Mesh, PartitionSpec as P

LOGIT_SCALE = 10.0
LOGIT_BIAS = -2.0
NORM_EPS = 1e-06

SIZES = {"zl": 2, "y": 4, "x": 4, "c": 2, "zh": 4}
DP = ("zl", "y", "x", "c")
LONG = pl.CostEstimate(flops=30_000_000_000, transcendentals=0, bytes_accessed=100_000_000)


def pulled(value, axis, steps):
    count = SIZES[axis]
    return lax.ppermute(value, axis, [((i + steps) % count, i) for i in range(count)])


def pulls(value, axis):
    return [value] + [pulled(value, axis, k) for k in (1, 2, 3)]


def ring(value, axis):
    half = value.shape[0] // 2
    up, down = pulled(value, axis, 1), pulled(value, axis, -1)
    return [value, up, pulled(up[:half], axis, 1), pulled(down[half:], axis, -1), down]


def ring_back(terms, axis):
    own, up, far_up, far_down, down = terms
    half = far_up.shape[0]
    up = jnp.concatenate([up[:half] + pulled(far_up, axis, -1), up[half:]])
    down = jnp.concatenate([down[:half], down[half:] + pulled(far_down, axis, 1)])
    return [own, pulled(up, axis, -1), pulled(down, axis, 1)]


def returned(terms, axis):
    return sum((pulled(terms[k], axis, -k) for k in (1, 2, 3)), terms[0])


def product(left, right, dims):
    return lax.dot_general(
        left,
        right,
        (dims, ((), ())),
        precision=lax.Precision.HIGHEST,
        preferred_element_type=jnp.float32,
    )


def unit_back(unit, scale, grad):
    return scale[:, None] * (grad - unit * jnp.sum(unit * grad, axis=1, keepdims=True))


def parts(value):
    high = value.astype(jnp.bfloat16)
    return high, (value - high.astype(jnp.float32)).astype(jnp.bfloat16)


def dot3(left, right, dims):
    def one(a, b):
        return lax.dot_general(a, b, (dims, ((), ())), preferred_element_type=jnp.float32)

    return one(left[0], right[0]) + (one(left[0], right[1]) + one(left[1], right[0]))


def image_kernel(own, other, wanted, held, *refs):
    blocks, grads, weights_out = refs[:10], refs[10:12], refs[12:]
    images = parts(jnp.concatenate([own[...], other[...]]))
    terms = 0.0
    for h, out in enumerate(weights_out):
        captions = parts(jnp.concatenate([r[...] for r in blocks[5 * h : 5 * h + 5]]))
        logits = LOGIT_SCALE * dot3(images, captions, ((1,), (1,))) + LOGIT_BIAS
        signs = jnp.where(wanted[:, :1] == held[h : h + 1, :], 1.0, -1.0).astype(jnp.float32)
        weights = (-LOGIT_SCALE * signs) * jax.nn.sigmoid(-signs * logits)
        out[...] = weights
        terms = terms + dot3(parts(weights), captions, ((1,), (0,)))
    size = own.shape[0]
    for k, ref in enumerate(grads):
        ref[...] = terms[k * size : (k + 1) * size]


def caption_kernel(own, other, weights, *sums):
    images = parts(jnp.concatenate([own[...], other[...]]))
    caption_terms = dot3(parts(weights[...].T), images, ((1,), (0,)))
    start = 0
    for ref in sums:
        ref[...] = caption_terms[start : start + ref.shape[0]]
        start += ref.shape[0]


def called(kernel, name, shapes, *args, cost=None):
    return pl.pallas_call(
        kernel,
        out_shape=[jax.ShapeDtypeStruct(shape, jnp.float32) for shape in shapes],
        compiler_params=pltpu.CompilerParams(vmem_limit_bytes=48 << 20),
        name=name,
        cost_estimate=cost,
    )(*args)


def image_terms(images, wanted, held, blocks):
    shapes = [images[0].shape] * 2 + [(wanted.shape[0], held.shape[1])] * 2
    out = called(image_kernel, "image_terms", shapes, *images, wanted, held, *blocks)
    return out[:2], out[2], out[3]


def caption_terms(images, weights, blocks, cost=None):
    shapes = [block.shape for block in blocks]
    return called(caption_kernel, "caption_terms", shapes, *images, weights, cost=cost)


def sum_kernel(*refs):
    refs[-1][...] = sum(ref[...] for ref in refs[:-1])


def summed(parts, cost=None):
    return called(sum_kernel, "line_sum", [parts[0].shape], *parts, cost=cost)[0]


def unit_kernel(raw, unit, scale):
    rows = raw[...]
    factor = lax.rsqrt(jnp.sum(rows * rows, axis=1, keepdims=True) + NORM_EPS)
    unit[...] = rows * factor
    scale[...] = jnp.broadcast_to(factor, scale.shape)


def image_unit_kernel(raw, unit, scale, sent):
    size = unit.shape[0]
    rows = sum(raw[k * size : (k + 1) * size] for k in range(4))
    factor = lax.rsqrt(jnp.sum(rows * rows, axis=1, keepdims=True) + NORM_EPS)
    unit[...] = rows * factor
    scale[...] = jnp.broadcast_to(factor, scale.shape)
    for k in range(4):
        sent[k * size : (k + 1) * size] = rows * factor


def raw_kernel(terms, unit, scale, sent):
    size = unit.shape[0]
    grad = sum(terms[k * size : (k + 1) * size] for k in range(4))
    dot = jnp.sum(unit[...] * grad, axis=1, keepdims=True)
    raw = scale[:, :1] * (grad - unit[...] * dot)
    for k in range(4):
        sent[k * size : (k + 1) * size] = raw


def line_parts(line):
    size = line.shape[0] // 4
    return [line[k * size : (k + 1) * size] for k in range(4)]


def local(pooled_rows, projection, text_rows, caption_row):
    zl, y, x, c, zh = (lax.axis_index(a) for a in ("zl", "y", "x", "c", "zh"))
    per_shard = pooled_rows.shape[0]
    count, width = text_rows.shape
    captions, caption_scale = called(
        unit_kernel, "caption_rows", [(count, width), (count, 128)], text_rows
    )

    partial = product(pooled_rows, projection, ((1,), (0,)))
    partial, moved = lax.optimization_barrier((partial, pulled(captions, "zl", 1)))
    arrived = lax.all_to_all(partial, "zh", 0, 0, tiled=True)

    near_line = jnp.concatenate(pulls(captions, "x"))
    far_line = jnp.concatenate(pulls(moved, "y"))
    near_line, far_line, arrived = lax.optimization_barrier((near_line, far_line, arrived))
    near = ring(near_line, "y")
    far = ring(far_line, "x")
    images, image_scale, sent = called(
        image_unit_kernel, "image_rows", [(count, width), (count, 128), partial.shape], arrived
    )
    shard_images = lax.all_to_all(sent, "zh", 0, 0, tiled=True)
    chip_images = [shard_images, pulled(shard_images, "c", 1)]

    named = caption_row.astype(jnp.float32)
    wanted = jnp.concatenate([named, pulled(named, "c", 1)])
    wanted = jnp.broadcast_to(wanted[:, None], (2 * per_shard, 128))

    steps = jnp.arange(4, dtype=jnp.int32)
    rows = jnp.arange(count, dtype=jnp.int32)

    def numbers(zl, y, x):
        shard = ((zl * 4 + y % 4) * 4 + x % 4) * 2 + c
        held = (shard * per_shard + zh * count)[:, :, None] + rows
        return held.reshape(1, -1).astype(jnp.float32)

    near_held = numbers(zl, (y + steps)[:, None], (x + steps)[None, :])
    far_held = numbers(1 - zl, (y + steps)[None, :], (x + steps)[:, None])

    held = jnp.concatenate([near_held, far_held])
    grads, near_weights, far_weights = image_terms(chip_images, wanted, held, [*near, *far])
    grads, far_weights = lax.optimization_barrier((grads, far_weights))
    far_sums = caption_terms(chip_images, far_weights, far[:1] * 4, cost=LONG)
    shard_grad = grads[0] + pulled(grads[1], "c", 1)
    shard_grad, near_weights = lax.optimization_barrier((shard_grad, near_weights))
    near_sums = caption_terms(chip_images, near_weights, near, cost=LONG)

    (sent,) = called(
        raw_kernel,
        "image_back",
        [shard_grad.shape],
        lax.all_to_all(shard_grad, "zh", 0, 0, tiled=True),
        images,
        image_scale,
    )
    near_parts = ring_back(near_sums, "y")
    far_parts = [far_sums[0]] + [pulled(far_sums[k], "x", -k) for k in (1, 2, 3)]
    raw_rows = lax.all_to_all(sent, "zh", 0, 0, tiled=True)

    far_parts, sent = lax.optimization_barrier((far_parts, sent))
    far_line = summed(far_parts, cost=LONG)
    near_parts, _ = lax.optimization_barrier((near_parts, far_line))
    far_own, *far_rest = line_parts(far_line)
    far_rest = [pulled(part, "y", -k) for k, part in enumerate(far_rest, 1)]
    far_own, raw_rows = lax.optimization_barrier((far_own, raw_rows))
    pooled_grad = product(raw_rows, projection, ((1,), (1,)))
    far_sum = sum(far_rest, far_own)
    near_sum = returned(line_parts(summed(near_parts)), "x")
    caption_grad = near_sum + pulled(far_sum, "zl", 1)
    text_grad = unit_back(captions, caption_scale[:, 0], caption_grad)
    return (pooled_grad, text_grad)


def solution(mesh):
    grid = Mesh(mesh.devices.reshape(tuple(SIZES.values())), tuple(SIZES))
    return jax.shard_map(
        local,
        mesh=grid,
        in_specs=(P(DP, "zh"), P("zh", None), P((*DP, "zh"), None), P(DP)),
        out_specs=(P(DP, "zh"), P((*DP, "zh"), None)),
        check_vma=False,
    )
```
